256 devices in a mesh: row: 8 (over x, y_hi), col: 32 (over z, y_lo, core).
Axes of the slice: x: 4, y: 4 (y_hi: 2, y_lo: 2; y = y_hi * 2 + y_lo), z: 8, core: 2. Of those that a mesh axis runs over, the one named last changes fastest.
Arguments:
- forward_state: bfloat16 [134217728], P(('row', 'col')), may hold values from -6 to 6
- adjoint_state: bfloat16 [134217728], P(('row', 'col')), may hold values from -6 to 6
- gate_matrix: bfloat16 [1024, 1024], replicated, may hold values from -1 to 1, as said below
Outputs:
- forward_final: bfloat16 [134217728], P(('row', 'col'))
- adjoint_final: bfloat16 [134217728], P(('row', 'col'))
- first_environment: float32 [1048576], P(('row', 'col'))
- second_environment: float32 [1048576], P(('row', 'col'))
The draws below stay inside these ranges and needn't reach their ends.
Inputs may be any that keep to these rules, and one draw needn't show every extreme that they name: `gate_matrix`: an orthogonal matrix rounded to bfloat16.
All inputs are finite; a program needn't handle non-finite values.
Results may differ from the reference program's by a relative error of at most 0.0057.
Values may be sent and summed in bfloat16 or wider, within the bound.
A program may use at most 128 MiB of HBM per device.

```python
import math
import jax
import jax.numpy as jnp
from jax import lax

GATE = 1024
AMP_DEV = 524288
AMPS = 134217728
N_ROW = 8
N_COL = 32


def draw_gate_matrix(key, part):
    sample = jax.random.normal(jax.random.fold_in(key, 7), (GATE, GATE), jnp.float32)
    orthogonal, triangle = jnp.linalg.qr(sample)
    sign_flip = jnp.where(jnp.diagonal(triangle) < 0, -1.0, 1.0)
    return (orthogonal * sign_flip[None, :]).astype(jnp.bfloat16)


def steps_of(rng, extent, shards, least, high):
    level = 1.0
    for position, blocks in shards:
        steps = jax.random.uniform(jax.random.fold_in(jax.random.fold_in(rng, 6), position), (blocks,), jnp.float32, least / len(shards), high / len(shards))
        level = level * jnp.repeat(jnp.exp(steps), extent[position] // blocks).reshape((-1,) + (1,) * (len(extent) - 1 - position))
    return level


def centred(rng, dims, spread, bound, pieces=(), dtype=jnp.bfloat16):
    result = jax.random.normal(rng, dims, jnp.float32) * spread
    if len(pieces) > 0:
        result = steps_of(rng, dims, pieces, -0.22, 0.18) * result
    return jnp.clip(result, min=-bound, max=bound).astype(dtype)


def setup_inputs(seed: int = 0) -> dict:
    key_of = jax.random.split(jax.random.key(seed), 4)
    return {
        "forward_state": centred(key_of[0], (AMPS,), 1.0, 6.0, ((0, 256),)),
        "adjoint_state": centred(key_of[1], (AMPS,), 1.0, 6.0, ((0, 256),)),
        "gate_matrix": draw_gate_matrix(jax.random.fold_in(key_of[3], 71), 0),
    }


def gate_layer(forward, adjoint, unitary, shape, move_form, env_form, scale):
    forward_grid = forward.astype(jnp.float32).reshape(shape)
    adjoint_grid = adjoint.astype(jnp.float32).reshape(shape)
    forward_next = jnp.einsum(move_form, unitary, forward_grid, precision=lax.Precision.HIGHEST).astype(jnp.bfloat16)
    adjoint_next = jnp.einsum(move_form, unitary, adjoint_grid, precision=lax.Precision.HIGHEST).astype(jnp.bfloat16)
    environment = jnp.einsum(env_form, adjoint_next.astype(jnp.float32), forward_grid, precision=lax.Precision.HIGHEST)
    environment = (environment * scale).reshape(GATE * GATE)
    return (forward_next.reshape(-1), adjoint_next.reshape(-1), environment)

def reference(forward_state, adjoint_state, gate_matrix):
    half_row = N_ROW // 2
    half_col = N_COL // 2
    quarter = GATE // 4
    columns = AMP_DEV // GATE
    unitary = gate_matrix.astype(jnp.float32).reshape(2, 2, quarter, 2, 2, quarter)
    scale = 1.0 / math.sqrt(N_ROW * N_COL * AMP_DEV / GATE)
    first_shape = (half_row, 2, 2, half_col, 4, quarter, columns)
    forward_mid, adjoint_mid, first_environment = gate_layer(forward_state, adjoint_state, unitary, first_shape, 'ijkIJK,hIJcpKm->hijcpkm', 'hijcpkm,hIJcpKm->ijkIJK', scale)
    second_shape = (half_row, 2, half_col, 2, 4, quarter, columns)
    forward_final, adjoint_final, second_environment = gate_layer(forward_mid, adjoint_mid, unitary, second_shape, 'ijkIJK,hIcJpKm->hicjpkm', 'hicjpkm,hIcJpKm->ijkIJK', scale)
    return (forward_final, adjoint_final, first_environment, second_environment)
```

```python
import math

import jax
import jax.numpy as jnp
from jax import lax
from jax.experimental import pallas as pl
from jax.experimental.pallas import tpu as pltpu
from jax.sharding import PartitionSpec as P

MESH = pl.DeviceIdType.MESH
BF = jnp.bfloat16
F32 = jnp.float32


def flip(bit, by):
    return 1 - bit if by else bit


def kernel(
    scale, f_in, a_in, g_in, f_out, a_out, e1_out, e2_out,
    gate, flat, tmp, x1, x2, sb, fin, acc, cs, cr, xs, xr, yb, yr, zb, zr, fb, lc, lr,
    load_sem, home_sem, ex_s, ex_r, co_s, co_r, fi_s, fi_r, cs_s, cs_r, xs_s, xs_r, ys_s, ys_r, zs_s, zs_r, lc_s, lc_r,
):
    row, col = lax.axis_index("row"), lax.axis_index("col")
    xa, xb, yh = lax.div(row, 4), lax.rem(lax.div(row, 2), 2), lax.rem(row, 2)
    zh, zm, zl = lax.div(col, 16), lax.rem(lax.div(col, 8), 2), lax.rem(lax.div(col, 4), 2)
    yl, k = lax.rem(lax.div(col, 2), 2), lax.rem(col, 2)
    oth = 1 - k

    def peer(dx=0, dy=0, dz=0, dk=0):
        return {
            "row": (flip(xa, dx & 2) * 2 + flip(xb, dx & 1)) * 2 + flip(yh, dy & 2),
            "col": ((flip(zh, dz & 4) * 2 + flip(zm, dz & 2)) * 2 + flip(zl, dz & 1)) * 4
            + flip(yl, dy & 1) * 2
            + flip(k, dk),
        }

    def remote(src, dst, send, recv, to):
        return pltpu.make_async_remote_copy(
            src_ref=src, dst_ref=dst, send_sem=send, recv_sem=recv, device_id=to, device_id_type=MESH
        )

    ins, outs, env_outs = (f_in, a_in), (f_out, a_out), (e1_out, e2_out)
    home = yh * 2 + zh

    group = [(r, c, d) for r in (0, 1) for c in (1, 0) for d in (0, 1) if r + c + d]
    friends = [peer(dy=2 * r, dz=4 * c, dk=d) for r, c, d in group]
    friends += [peer(dx=d) for d in (1, 2, 3)] + [peer(dy=d) for d in (1, 3)]
    friends += [peer(dz=d) for d in (1, 2, 3, 5, 6, 7)]
    barrier = pltpu.get_barrier_semaphore()
    for friend in friends:
        pl.semaphore_signal(barrier, inc=1, device_id=friend, device_id_type=MESH)

    loads = [pltpu.make_async_copy(g_in, gate, load_sem.at[2])]
    for s in (0, 1):
        loads.append(pltpu.make_async_copy(ins[s].at[home], flat.at[s, home], load_sem.at[s]))
    for one in loads:
        one.start()
    pl.semaphore_wait(barrier, len(friends))

    steps = ((0, 1), (1, 1), (1, 0))
    first = {}
    for s in (0, 1):
        for j, (r, c) in enumerate(steps):
            quarter = flip(yh, r) * 2 + flip(zh, c)
            first[s, j] = remote(
                ins[s].at[quarter], flat.at[s, home], ex_s.at[s, j], ex_r.at[s, j], peer(dy=2 * r, dz=4 * c)
            )
            first[s, j].start()

    def untangle(s, slot):
        tmp[...] = flat[s, slot].astype(F32)
        rows = pl.ds(pl.multiple_of(slot * 256, 256), 256)
        for m in range(4):
            x1[s, m // 2, rows, (m % 2) * 128 : (m % 2) * 128 + 128] = tmp[pl.ds(m, 256, stride=4), :].astype(BF)

    def gather(s):
        loads[1 + s].wait()
        untangle(s, home)
        for j in (2, 0, 1):
            r, c = steps[j]
            first[s, j].wait_recv()
            untangle(s, flip(yh, r) * 2 + flip(zh, c))

    def block(i):
        return pl.ds(pl.multiple_of(i * 256, 256), 256)

    swaps = {}

    def gate_one(s):
        def other(i, carry):
            sb[s, i] = jnp.dot(gate[block(i), :], x1[s, oth], preferred_element_type=F32).astype(BF)
            return carry

        lax.fori_loop(0, 4, other, 0)
        for i in range(4):
            swaps[s, i] = remote(
                sb.at[s, i],
                x2.at[s, i % 2, block((i // 2) * 2 + k), :],
                co_s.at[s, i],
                co_r.at[s, i],
                peer(dk=1),
            )
            swaps[s, i].start()

        def own(i, carry):
            x2[s, lax.rem(i, 2), block(lax.div(i, 2) * 2 + k), :] = jnp.dot(
                gate[block(i), :], x1[s, k], preferred_element_type=F32
            ).astype(BF)
            return carry

        lax.fori_loop(0, 4, own, 0)

    last, homes = {}, []

    def gate_two(s):
        for i in range(4):
            swaps[s, i].wait_recv()
        for c in (1, 0):
            top = flip(zh, c)

            def apply(i, carry):
                fin[s, top, block(i), :] = jnp.dot(
                    gate[block(i), :], x2[s, top], preferred_element_type=F32
                ).astype(BF)
                return carry

            lax.fori_loop(0, 4, apply, 0)
            for r in (1, 0):
                for d in (0, 1):
                    src = fin.at[s, top, block(flip(yh, r) * 2 + flip(k, d)), :]
                    dst = outs[s].at[home, :, block(k)]
                    if r + c + d == 0:
                        one = pltpu.make_async_copy(src, dst, home_sem.at[s])
                        homes.append(one)
                    else:
                        j = group.index((r, c, d))
                        one = remote(src, dst, fi_s.at[s, j], fi_r.at[s, j], peer(dy=2 * r, dz=4 * c, dk=d))
                        last[s, j] = one
                    one.start()

    def outer(a, b):
        return lax.dot_general(a, b, (((1,), (1,)), ((), ())), preferred_element_type=F32)

    pairs = {}

    def half(i):
        return pl.ds(pl.multiple_of(i * 512, 512), 512)

    def env_blocks(e, left, right):
        def one(t, carry):
            d = lax.rem(t + 1, 4)
            da, db = lax.div(d, 2), lax.rem(d, 2)
            ia, ib = xa + da - 2 * xa * da, xb + db - 2 * xb * db
            lo, hi = left(ia, ib)
            cs[e, d] = (outer(lo, right(0, oth)) + outer(hi, right(1, oth))).astype(BF)
            acc[e, d] = outer(lo, right(0, k)) + outer(hi, right(1, k))
            return carry

        lax.fori_loop(0, 4, one, 0)
        for d in (1, 2, 3, 0):
            pairs[e, d] = remote(cs.at[e, d], cr.at[e, d], cs_s.at[e, d], cs_r.at[e, d], peer(dk=1))
            pairs[e, d].start()

    def env_one():
        env_blocks(
            0,
            lambda ia, ib: (sb[1, ia * 2 + ib], x2[1, ib, block(ia * 2 + k), :]),
            lambda m, h: x1[0, oth if m == 0 else k, half(h), :],
        )

    def env_two():
        env_blocks(
            1,
            lambda ia, ib: (fin[1, 0, block(ia * 2 + ib), :], fin[1, 1, block(ia * 2 + ib), :]),
            lambda m, h: x2[0, m, half(h), :],
        )

    xsend, ysend, zsend, csend = {}, {}, {}, {}

    def stage_x(e):
        for d in (1, 2, 3):
            pairs[e, d].wait_recv()
            xs[e, d - 1] = (acc[e, d] + cr[e, d].astype(F32)).astype(BF)
            xsend[e, d] = remote(xs.at[e, d - 1], xr.at[e, d - 1], xs_s.at[e, d - 1], xs_r.at[e, d - 1], peer(dx=d))
            xsend[e, d].start()
        pairs[e, 0].wait_recv()

    def stage_y(e):
        for d in (1, 2, 3):
            xsend[e, d].wait_recv()

        def gather_rows(t, carry):
            rows = pl.ds(pl.multiple_of(t * 16, 16), 16)
            total = acc[e, 0, rows, :] + cr[e, 0, rows, :].astype(F32)
            for j in range(3):
                total = total + xr[e, j, rows, :].astype(F32)
            y, z = lax.div(t, 8), lax.rem(t, 8)
            yb[e, y * 2, z] = total[:8]
            yb[e, y * 2 + 1, z] = total[8:]
            return carry

        lax.fori_loop(0, 16, gather_rows, 0)
        for d in (2, 1, 3):
            ysend[e, d] = remote(
                yb.at[e, flip(yh, d & 2) * 2 + flip(yl, d & 1)],
                yr.at[e, d - 1],
                ys_s.at[e, d - 1],
                ys_r.at[e, d - 1],
                peer(dy=d),
            )
            ysend[e, d].start()

    def stage_z(e):
        for d in (1, 2, 3):
            ysend[e, d].wait_recv()
        zb[e] = yb[e, yh * 2 + yl] + yr[e, 0] + yr[e, 1] + yr[e, 2]
        for d in (4, 5, 3, 6, 2, 7, 1):
            zsend[e, d] = remote(
                zb.at[e, (flip(zh, d & 4) * 2 + flip(zm, d & 2)) * 2 + flip(zl, d & 1)],
                zr.at[e, d - 1],
                zs_s.at[e, d - 1],
                zs_r.at[e, d - 1],
                peer(dz=d),
            )
            zsend[e, d].start()

    def stage_core(e):
        for d in range(1, 8):
            zsend[e, d].wait_recv()
        total = zb[e, (zh * 2 + zm) * 2 + zl]
        for d in range(7):
            total = total + zr[e, d]
        for j in range(4):
            fb[e, j * 8 : j * 8 + 8, :] = total[:, j * 128 : j * 128 + 128] * scale
        for j in range(4):
            lc[e, j * 4 : j * 4 + 4, :] = fb[e, pl.ds(j * 8 + oth * 4, 4), :]
            env_outs[e][pl.ds(k * 4 + j, 4, stride=8), :] = fb[e, pl.ds(j * 8 + k * 4, 4), :]
        csend[e] = remote(lc.at[e], lr.at[e], lc_s.at[e], lc_r.at[e], peer(dk=1))
        csend[e].start()

    def stage_end(e):
        csend[e].wait_recv()
        for j in range(4):
            env_outs[e][pl.ds(oth * 4 + j, 4, stride=8), :] = lr[e, j * 4 : j * 4 + 4, :]

    loads[0].wait()
    gather(0)
    gate_one(0)
    gate_two(0)
    gather(1)
    gate_one(1)
    env_one()
    gate_two(1)
    env_two()
    stage_x(0)
    stage_x(1)
    stage_y(0)
    stage_z(0)
    stage_y(1)
    stage_z(1)
    stage_core(0)
    stage_core(1)
    stage_end(0)
    stage_end(1)
    for one in last.values():
        one.wait_recv()
    for one in homes:
        one.wait()
    for sent in (first, swaps, last, pairs, xsend, ysend, zsend, csend):
        for one in sent.values():
            one.wait_send()


def on_device(forward_state, adjoint_state, gate_matrix):
    scale = 1.0 / math.sqrt(lax.axis_size("row") * lax.axis_size("col") * forward_state.shape[0] / gate_matrix.shape[0])
    dma = pltpu.SemaphoreType.DMA
    any_space = pl.BlockSpec(memory_space=pl.ANY)
    vmem = pl.BlockSpec(memory_space=pltpu.VMEM)
    scratch = [
        ((1024, 1024), BF),
        ((2, 4, 1024, 128), BF),
        ((1024, 128), F32),
        ((2, 2, 1024, 256), BF),
        ((2, 2, 1024, 256), BF),
        ((2, 4, 256, 256), BF),
        ((2, 2, 1024, 256), BF),
        ((2, 4, 256, 512), F32),
        ((2, 4, 256, 512), BF),
        ((2, 4, 256, 512), BF),
        ((2, 3, 256, 512), BF),
        ((2, 3, 256, 512), BF),
        ((2, 4, 8, 8, 512), F32),
        ((2, 3, 8, 8, 512), F32),
        ((2, 8, 8, 512), F32),
        ((2, 7, 8, 512), F32),
        ((2, 32, 128), F32),
        ((2, 16, 128), F32),
        ((2, 16, 128), F32),
    ]
    sems = [(3,), (2,)]
    for shape in ((2, 3), (2, 4), (2, 7), (2, 4), (2, 3), (2, 3), (2, 7), (2,)):
        sems += [shape, shape]
    outs = pl.pallas_call(
        lambda *refs: kernel(scale, *refs),
        out_shape=[
            jax.ShapeDtypeStruct((4, 256, 512), BF),
            jax.ShapeDtypeStruct((4, 256, 512), BF),
            jax.ShapeDtypeStruct((32, 128), F32),
            jax.ShapeDtypeStruct((32, 128), F32),
        ],
        in_specs=[any_space] * 3,
        out_specs=[any_space, any_space, vmem, vmem],
        scratch_shapes=[pltpu.VMEM(shape, kind) for shape, kind in scratch] + [dma(shape) for shape in sems],
        compiler_params=pltpu.CompilerParams(collective_id=0, has_side_effects=True),
        name="step",
    )(forward_state.reshape(4, 1024, 128), adjoint_state.reshape(4, 1024, 128), gate_matrix)
    return tuple(one.reshape(-1) for one in outs)


def solution(mesh):
    spec = P(("row", "col"))
    return jax.shard_map(
        on_device, mesh=mesh, in_specs=(spec, spec, P()), out_specs=(spec, spec, spec, spec), check_vma=False
    )
```

```python
import math

import jax
import jax.numpy as jnp
from jax import lax
from jax.experimental import pallas as pl
from jax.experimental.pallas import tpu as pltpu
from jax.sharding import PartitionSpec as P

MESH = pl.DeviceIdType.MESH
BF = jnp.bfloat16
F32 = jnp.float32


def flip(bit, by):
    return 1 - bit if by else bit


def kernel(
    scale, f_in, a_in, g_in, f_out, a_out, e1_out, e2_out,
    gate, flat, legs, legs2, tmp, x1, x2, sb, fin, ac0, ac1, mid, cs, cr, xs, xr, ys, yr, ys2, yr2, xs2, xr2, zb, zs, zr, fb, lc, lr,
    load_sem, home_sem, ex_s, ex_r, le_s, le_r, le2_s, le2_r, co_s, co_r, fi_s, fi_r, cs_s, cs_r, xs_s, xs_r, ys_s, ys_r,
    ys2_s, ys2_r, xs2_s, xs2_r, zs_s, zs_r, lc_s, lc_r,
):
    row, col = lax.axis_index("row"), lax.axis_index("col")
    xa, xb, yh = lax.div(row, 4), lax.rem(lax.div(row, 2), 2), lax.rem(row, 2)
    zh, zm, zl = lax.div(col, 16), lax.rem(lax.div(col, 8), 2), lax.rem(lax.div(col, 4), 2)
    yl, k = lax.rem(lax.div(col, 2), 2), lax.rem(col, 2)
    oth = 1 - k

    def peer(dx=0, dy=0, dz=0, dk=0):
        return {
            "row": (flip(xa, dx & 2) * 2 + flip(xb, dx & 1)) * 2 + flip(yh, dy & 2),
            "col": ((flip(zh, dz & 4) * 2 + flip(zm, dz & 2)) * 2 + flip(zl, dz & 1)) * 4
            + flip(yl, dy & 1) * 2
            + flip(k, dk),
        }

    def remote(src, dst, send, recv, to):
        return pltpu.make_async_remote_copy(
            src_ref=src, dst_ref=dst, send_sem=send, recv_sem=recv, device_id=to, device_id_type=MESH
        )

    ins, outs, env_outs = (f_in, a_in), (f_out, a_out), (e1_out, e2_out)
    home = yh * 2 + zh

    group = [(r, c, d) for r in (0, 1) for c in (1, 0) for d in (0, 1) if r + c + d]
    friends = [peer(dy=2 * r, dz=4 * c, dk=d) for r, c, d in group]
    friends += [peer(dx=d) for d in (1, 2, 3)] + [peer(dy=d) for d in (1, 3)]
    friends += [peer(dz=d) for d in (1, 2, 3, 5, 6, 7)]
    barrier = pltpu.get_barrier_semaphore()
    for friend in friends:
        pl.semaphore_signal(barrier, inc=1, device_id=friend, device_id_type=MESH)

    loads = [pltpu.make_async_copy(g_in, gate, load_sem.at[2])]
    for s in (0, 1):
        loads.append(pltpu.make_async_copy(ins[s].at[home], flat.at[s, home], load_sem.at[s]))
    for one in loads:
        one.start()
    pl.semaphore_wait(barrier, len(friends))

    steps = ((0, 1), (1, 1), (1, 0))
    first, relays = {}, {}

    def quarter(r, c):
        return flip(yh, r) * 2 + flip(zh, c)

    def open_leg(s):
        relays[s] = remote(ins[s].at[quarter(1, 1)], legs.at[s], le_s.at[s], le_r.at[s], peer(dy=2))
        relays[s].start()

    def open_direct(s, j):
        r, c = steps[j]
        first[s, j] = remote(
            ins[s].at[quarter(r, c)], flat.at[s, home], ex_s.at[s, j], ex_r.at[s, j], peer(dy=2 * r, dz=4 * c)
        )
        first[s, j].start()

    def open_relay(s):
        relays[s].wait_recv()
        first[s, 1] = remote(legs.at[s], flat.at[s, quarter(1, 0)], ex_s.at[s, 1], ex_r.at[s, 1], peer(dz=4))
        first[s, 1].start()

    open_direct(0, 0)
    open_leg(0)
    open_leg(1)
    open_direct(0, 2)
    open_direct(1, 2)
    open_relay(0)
    open_direct(1, 0)
    open_relay(1)

    def untangle(s, slot):
        tmp[...] = flat[s, slot].astype(F32)
        rows = pl.ds(pl.multiple_of(slot * 256, 256), 256)
        for m in range(4):
            x1[s, m // 2, rows, (m % 2) * 128 : (m % 2) * 128 + 128] = tmp[pl.ds(m, 256, stride=4), :].astype(BF)

    def gather(s, j):
        if j < 0:
            loads[1 + s].wait()
            untangle(s, home)
        else:
            first[s, j].wait_recv()
            untangle(s, quarter(*steps[j]))

    def block(i):
        return pl.ds(pl.multiple_of(i * 256, 256), 256)

    swaps = {}

    def gate_one(s):
        def other(i, carry):
            sb[s, i] = jnp.dot(gate[block(i), :], x1[s, oth], preferred_element_type=F32).astype(BF)
            return carry

        lax.fori_loop(0, 4, other, 0)
        for i in range(4):
            swaps[s, i] = remote(
                sb.at[s, i],
                x2.at[s, i % 2, block((i // 2) * 2 + k), :],
                co_s.at[s, i],
                co_r.at[s, i],
                peer(dk=1),
            )
            swaps[s, i].start()

        def own(i, carry):
            x2[s, lax.rem(i, 2), block(lax.div(i, 2) * 2 + k), :] = jnp.dot(
                gate[block(i), :], x1[s, k], preferred_element_type=F32
            ).astype(BF)
            return carry

        lax.fori_loop(0, 4, own, 0)

    last, relays2, homes = {}, {}, []

    def piece(s, r, c, d):
        return fin.at[s, flip(zh, c), block(flip(yh, r) * 2 + flip(k, d)), :]

    def close_leg(s):
        for d in (0, 1):
            relays2[s, d] = remote(piece(s, 1, 1, d), legs2.at[s, d], le2_s.at[s, d], le2_r.at[s, d], peer(dy=2))
            relays2[s, d].start()

    def close(s, r, c, d):
        dst = outs[s].at[home, :, block(k)]
        if r + c + d == 0:
            one = pltpu.make_async_copy(piece(s, r, c, d), dst, home_sem.at[s])
            homes.append(one)
        else:
            j = group.index((r, c, d))
            one = remote(piece(s, r, c, d), dst, fi_s.at[s, j], fi_r.at[s, j], peer(dy=2 * r, dz=4 * c, dk=d))
            last[s, j] = one
        one.start()

    def close_relay(s, d):
        j = group.index((1, 1, d))
        relays2[s, d].wait_recv()
        last[s, j] = remote(
            legs2.at[s, d],
            outs[s].at[quarter(1, 0), :, block(k)],
            fi_s.at[s, j],
            fi_r.at[s, j],
            peer(dz=4, dk=d),
        )
        last[s, j].start()

    def gate_two(s, c):
        top = flip(zh, c)

        def apply(i, carry):
            fin[s, top, block(i), :] = jnp.dot(gate[block(i), :], x2[s, top], preferred_element_type=F32).astype(BF)
            return carry

        lax.fori_loop(0, 4, apply, 0)

    def swapped(s):
        for i in range(4):
            swaps[s, i].wait_recv()

    def outer(a, b):
        return lax.dot_general(a, b, (((1,), (1,)), ((), ())), preferred_element_type=F32)

    pairs = {}

    def half(i):
        return pl.ds(pl.multiple_of(i * 512, 512), 512)

    def env_blocks(e, left, right):
        def one(t, carry):
            d = lax.rem(t + 1, 4)
            da, db = lax.div(d, 2), lax.rem(d, 2)
            ia, ib = xa + da - 2 * xa * da, xb + db - 2 * xb * db
            lo, hi = left(ia, ib)
            cs[e, d] = (outer(lo, right(0, oth)) + outer(hi, right(1, oth))).astype(BF)
            keep = outer(lo, right(0, k)) + outer(hi, right(1, k))
            ac0[e, d] = keep[:, :256]
            ac1[e, d] = keep[:, 256:].reshape(2, 8, 2, 8, 256)
            return carry

        lax.fori_loop(0, 4, one, 0)
        for d in (1, 2, 3, 0):
            pairs[e, d] = remote(cs.at[e, d], cr.at[e, d], cs_s.at[e, d], cs_r.at[e, d], peer(dk=1))
            pairs[e, d].start()

    def env_one():
        env_blocks(
            0,
            lambda ia, ib: (sb[1, ia * 2 + ib], x2[1, ib, block(ia * 2 + k), :]),
            lambda m, h: x1[0, oth if m == 0 else k, half(h), :],
        )

    def env_two():
        env_blocks(
            1,
            lambda ia, ib: (fin[1, 0, block(ia * 2 + ib), :], fin[1, 1, block(ia * 2 + ib), :]),
            lambda m, h: x2[0, m, half(h), :],
        )

    xsend, ysend, ysend2, xsend2, zsend, csend = {}, {}, {}, {}, {}, {}

    def push(table, e, d, src, dst, send, recv, to):
        table[e, d] = remote(src.at[e, d - 1], dst.at[e, d - 1], send.at[e, d - 1], recv.at[e, d - 1], to)
        table[e, d].start()

    def wait_all(table, e):
        for d in (1, 2, 3):
            table[e, d].wait_recv()

    def rows_of(d):
        return flip(yh, d & 2), flip(yl, d & 1)

    def stage_one(e):
        for d in (2, 1, 3, 0):
            pairs[e, d].wait_recv()
            first_half = ac0[e, d] + cr[e, d, :, :256].astype(F32)
            if d:
                xs[e, d - 1] = first_half.astype(BF)
                push(xsend, e, d, xs, xr, xs_s, xs_r, peer(dx=d))
            else:
                ac0[e, 0] = first_half
            ac1[e, d] += cr[e, d, :, 256:].astype(F32).reshape(2, 8, 2, 8, 256)
        for d in (2, 1, 3):
            a, b = rows_of(d)
            for i in range(4):
                ys[e, d - 1, i] = ac1[e, i, a, :, b].reshape(64, 256).astype(BF)
            push(ysend, e, d, ys, yr, ys_s, ys_r, peer(dy=d))

    def stage_two(e):
        wait_all(xsend, e)
        total = ac0[e, 0]
        for j in range(3):
            total = total + xr[e, j].astype(F32)
        mid[e] = total.reshape(2, 8, 2, 8, 256)
        for d in (2, 1, 3):
            a, b = rows_of(d)
            ys2[e, d - 1] = mid[e, a, :, b].reshape(64, 256).astype(BF)
            push(ysend2, e, d, ys2, yr2, ys2_s, ys2_r, peer(dy=d))
        wait_all(ysend, e)
        for d in (2, 1, 3, 0):
            total = ac1[e, d, yh, :, yl].reshape(64, 256)
            for j in range(3):
                total = total + yr[e, j, d].astype(F32)
            if d:
                xs2[e, d - 1] = total.astype(BF)
                push(xsend2, e, d, xs2, xr2, xs2_s, xs2_r, peer(dx=d))
            else:
                zb[e, :, 8:, :] = total.reshape(8, 8, 256)

    def stage_z(e):
        wait_all(ysend2, e)
        total = mid[e, yh, :, yl].reshape(64, 256)
        for j in range(3):
            total = total + yr2[e, j].astype(F32)
        zb[e, :, :8, :] = total.reshape(8, 8, 256)
        wait_all(xsend2, e)
        total = zb[e, :, 8:, :].reshape(64, 256)
        for j in range(3):
            total = total + xr2[e, j].astype(F32)
        zb[e, :, 8:, :] = total.reshape(8, 8, 256)
        zs[e] = zb[e].astype(BF)
        for d in (4, 5, 3, 6, 2, 7, 1):
            zsend[e, d] = remote(
                zs.at[e, (flip(zh, d & 4) * 2 + flip(zm, d & 2)) * 2 + flip(zl, d & 1)],
                zr.at[e, d - 1],
                zs_s.at[e, d - 1],
                zs_r.at[e, d - 1],
                peer(dz=d),
            )
            zsend[e, d].start()

    def stage_core(e):
        for d in range(1, 8):
            zsend[e, d].wait_recv()
        total = zb[e, (zh * 2 + zm) * 2 + zl]
        for d in range(7):
            total = total + zr[e, d].astype(F32)
        total = total * scale
        for j in range(4):
            q, c = j // 2, j % 2
            fb[e, j * 8 : j * 8 + 8, :] = total[q * 8 : q * 8 + 8, c * 128 : c * 128 + 128]
        for j in range(4):
            lc[e, j * 4 : j * 4 + 4, :] = fb[e, pl.ds(j * 8 + oth * 4, 4), :]
            env_outs[e][pl.ds(k * 4 + j, 4, stride=8), :] = fb[e, pl.ds(j * 8 + k * 4, 4), :]
        csend[e] = remote(lc.at[e], lr.at[e], lc_s.at[e], lc_r.at[e], peer(dk=1))
        csend[e].start()

    def stage_end(e):
        csend[e].wait_recv()
        for j in range(4):
            env_outs[e][pl.ds(oth * 4 + j, 4, stride=8), :] = lr[e, j * 4 : j * 4 + 4, :]

    gather(0, -1)
    gather(1, -1)
    loads[0].wait()
    gather(0, 2)
    gather(0, 0)
    gather(0, 1)
    gate_one(0)
    swapped(0)
    gate_two(0, 1)
    close(0, 0, 1, 0)
    close(0, 0, 1, 1)
    close_leg(0)
    gate_two(0, 0)
    for r, d in ((1, 0), (1, 1), (0, 1), (0, 0)):
        close(0, r, 0, d)
    gather(1, 2)
    close_relay(0, 0)
    close_relay(0, 1)
    gather(1, 0)
    gather(1, 1)
    gate_one(1)
    env_one()
    swapped(1)
    gate_two(1, 1)
    close(1, 0, 1, 0)
    close(1, 0, 1, 1)
    close_leg(1)
    gate_two(1, 0)
    stage_one(0)
    env_two()
    close_relay(1, 0)
    stage_one(1)
    stage_two(0)
    stage_two(1)
    for r, d in ((1, 0), (1, 1), (0, 1), (0, 0)):
        close(1, r, 0, d)
    stage_z(0)
    stage_z(1)
    close_relay(1, 1)
    stage_core(0)
    stage_core(1)
    stage_end(0)
    stage_end(1)
    for one in last.values():
        one.wait_recv()
    for one in homes:
        one.wait()
    for sent in (first, relays, relays2, swaps, last, pairs, xsend, ysend, ysend2, xsend2, zsend, csend):
        for one in sent.values():
            one.wait_send()


def on_device(forward_state, adjoint_state, gate_matrix):
    scale = 1.0 / math.sqrt(lax.axis_size("row") * lax.axis_size("col") * forward_state.shape[0] / gate_matrix.shape[0])
    dma = pltpu.SemaphoreType.DMA
    any_space = pl.BlockSpec(memory_space=pl.ANY)
    vmem = pl.BlockSpec(memory_space=pltpu.VMEM)
    scratch = [
        ((1024, 1024), BF),
        ((2, 4, 1024, 128), BF),
        ((2, 1024, 128), BF),
        ((2, 2, 256, 256), BF),
        ((1024, 128), F32),
        ((2, 2, 1024, 256), BF),
        ((2, 2, 1024, 256), BF),
        ((2, 4, 256, 256), BF),
        ((2, 2, 1024, 256), BF),
        ((2, 4, 256, 256), F32),
        ((2, 4, 2, 8, 2, 8, 256), F32),
        ((2, 2, 8, 2, 8, 256), F32),
        ((2, 4, 256, 512), BF),
        ((2, 4, 256, 512), BF),
        ((2, 3, 256, 256), BF),
        ((2, 3, 256, 256), BF),
        ((2, 3, 4, 64, 256), BF),
        ((2, 3, 4, 64, 256), BF),
        ((2, 3, 64, 256), BF),
        ((2, 3, 64, 256), BF),
        ((2, 3, 64, 256), BF),
        ((2, 3, 64, 256), BF),
        ((2, 8, 16, 256), F32),
        ((2, 8, 16, 256), BF),
        ((2, 7, 16, 256), BF),
        ((2, 32, 128), F32),
        ((2, 16, 128), F32),
        ((2, 16, 128), F32),
    ]
    sems = [(3,), (2,)]
    for shape in ((2, 3), (2,), (2, 2), (2, 4), (2, 7), (2, 4), (2, 3), (2, 3), (2, 3), (2, 3), (2, 7), (2,)):
        sems += [shape, shape]
    outs = pl.pallas_call(
        lambda *refs: kernel(scale, *refs),
        out_shape=[
            jax.ShapeDtypeStruct((4, 256, 512), BF),
            jax.ShapeDtypeStruct((4, 256, 512), BF),
            jax.ShapeDtypeStruct((32, 128), F32),
            jax.ShapeDtypeStruct((32, 128), F32),
        ],
        in_specs=[any_space] * 3,
        out_specs=[any_space, any_space, vmem, vmem],
        scratch_shapes=[pltpu.VMEM(shape, kind) for shape, kind in scratch] + [dma(shape) for shape in sems],
        compiler_params=pltpu.CompilerParams(collective_id=0, has_side_effects=True),
        name="step",
    )(forward_state.reshape(4, 1024, 128), adjoint_state.reshape(4, 1024, 128), gate_matrix)
    return tuple(one.reshape(-1) for one in outs)


def solution(mesh):
    spec = P(("row", "col"))
    return jax.shard_map(
        on_device, mesh=mesh, in_specs=(spec, spec, P()), out_specs=(spec, spec, spec, spec), check_vma=False
    )
```

```python
import math

import jax
import jax.numpy as jnp
from jax import lax
from jax.experimental import pallas as pl
from jax.experimental.pallas import tpu as pltpu
from jax.sharding import PartitionSpec as P

MESH = pl.DeviceIdType.MESH
BF = jnp.bfloat16
F32 = jnp.float32


def flip(bit, by):
    return 1 - bit if by else bit


def kernel(
    scale, f_in, a_in, g_in, f_out, a_out, e1_out, e2_out,
    gate, flat, legs, legs2, tmp, x1, x2, sb, fin, ac0, ac1, mid, cs, cr, xs, xr, ys, yr, ys2, yr2, xs2, xr2, zb, zs, zr, fb, lc, lr,
    load_sem, home_sem, ex_s, ex_r, le_s, le_r, le2_s, le2_r, co_s, co_r, fi_s, fi_r, cs_s, cs_r, xs_s, xs_r, ys_s, ys_r,
    ys2_s, ys2_r, xs2_s, xs2_r, zs_s, zs_r, lc_s, lc_r,
):
    row, col = lax.axis_index("row"), lax.axis_index("col")
    xa, xb, yh = lax.div(row, 4), lax.rem(lax.div(row, 2), 2), lax.rem(row, 2)
    zh, zm, zl = lax.div(col, 16), lax.rem(lax.div(col, 8), 2), lax.rem(lax.div(col, 4), 2)
    yl, k = lax.rem(lax.div(col, 2), 2), lax.rem(col, 2)
    oth = 1 - k

    def peer(dx=0, dy=0, dz=0, dk=0):
        return {
            "row": (flip(xa, dx & 2) * 2 + flip(xb, dx & 1)) * 2 + flip(yh, dy & 2),
            "col": ((flip(zh, dz & 4) * 2 + flip(zm, dz & 2)) * 2 + flip(zl, dz & 1)) * 4
            + flip(yl, dy & 1) * 2
            + flip(k, dk),
        }

    def remote(src, dst, send, recv, to):
        return pltpu.make_async_remote_copy(
            src_ref=src, dst_ref=dst, send_sem=send, recv_sem=recv, device_id=to, device_id_type=MESH
        )

    ins, outs, env_outs = (f_in, a_in), (f_out, a_out), (e1_out, e2_out)
    home = yh * 2 + zh

    group = [(r, c, d) for r in (0, 1) for c in (1, 0) for d in (0, 1) if r + c + d]
    friends = [peer(dy=2 * r, dz=4 * c, dk=d) for r, c, d in group if r + c < 2]
    friends += [peer(dx=d) for d in (1, 2, 3)] + [peer(dy=d) for d in (1, 3)]
    friends += [peer(dz=d) for d in (1, 2, 3, 5, 6, 7)]
    barrier = pltpu.get_barrier_semaphore()
    for friend in friends:
        pl.semaphore_signal(barrier, inc=1, device_id=friend, device_id_type=MESH)

    loads = [pltpu.make_async_copy(g_in, gate, load_sem.at[2])]
    for s in (0, 1):
        loads.append(pltpu.make_async_copy(ins[s].at[home], flat.at[s, home], load_sem.at[s]))
    for one in loads:
        one.start()
    pl.semaphore_wait(barrier, len(friends))

    steps = ((0, 1), (1, 1), (1, 0))
    first, relays = {}, {}

    def quarter(r, c):
        return flip(yh, r) * 2 + flip(zh, c)

    def open_leg(s):
        relays[s] = remote(ins[s].at[quarter(1, 1)], legs.at[s], le_s.at[s], le_r.at[s], peer(dy=2))
        relays[s].start()

    def open_direct(s, j):
        r, c = steps[j]
        first[s, j] = remote(
            ins[s].at[quarter(r, c)], flat.at[s, home], ex_s.at[s, j], ex_r.at[s, j], peer(dy=2 * r, dz=4 * c)
        )
        first[s, j].start()

    def open_relay(s):
        relays[s].wait_recv()
        first[s, 1] = remote(legs.at[s], flat.at[s, quarter(1, 0)], ex_s.at[s, 1], ex_r.at[s, 1], peer(dz=4))
        first[s, 1].start()

    open_direct(0, 0)
    open_leg(0)
    open_leg(1)
    open_direct(0, 2)
    open_direct(1, 2)
    open_direct(1, 0)
    open_relay(0)
    open_relay(1)

    def untangle(s, slot):
        tmp[...] = flat[s, slot].astype(F32)
        rows = pl.ds(pl.multiple_of(slot * 256, 256), 256)
        for m in range(4):
            x1[s, m // 2, rows, (m % 2) * 128 : (m % 2) * 128 + 128] = tmp[pl.ds(m, 256, stride=4), :].astype(BF)

    def gather(s, j):
        if j < 0:
            loads[1 + s].wait()
            untangle(s, home)
        else:
            first[s, j].wait_recv()
            untangle(s, quarter(*steps[j]))

    def block(i):
        return pl.ds(pl.multiple_of(i * 256, 256), 256)

    swaps = {}

    def gate_one(s):
        def other(i, carry):
            sb[s, i] = jnp.dot(gate[block(i), :], x1[s, oth], preferred_element_type=F32).astype(BF)
            return carry

        lax.fori_loop(0, 4, other, 0)
        for i in range(4):
            swaps[s, i] = remote(
                sb.at[s, i],
                x2.at[s, i % 2, block((i // 2) * 2 + k), :],
                co_s.at[s, i],
                co_r.at[s, i],
                peer(dk=1),
            )
            swaps[s, i].start()

        def own(i, carry):
            x2[s, lax.rem(i, 2), block(lax.div(i, 2) * 2 + k), :] = jnp.dot(
                gate[block(i), :], x1[s, k], preferred_element_type=F32
            ).astype(BF)
            return carry

        lax.fori_loop(0, 4, own, 0)

    last, relays2, homes = {}, {}, []

    def piece(s, r, c, d):
        return fin.at[s, flip(zh, c), block(flip(yh, r) * 2 + flip(k, d)), :]

    def close_leg(s):
        for d in (0, 1):
            relays2[s, d] = remote(piece(s, 1, 1, d), legs2.at[s, d], le2_s.at[s, d], le2_r.at[s, d], peer(dy=2))
            relays2[s, d].start()

    def close(s, r, c, d):
        dst = outs[s].at[home, :, block(k)]
        if r + c + d == 0:
            one = pltpu.make_async_copy(piece(s, r, c, d), dst, home_sem.at[s])
            homes.append(one)
        else:
            j = group.index((r, c, d))
            one = remote(piece(s, r, c, d), dst, fi_s.at[s, j], fi_r.at[s, j], peer(dy=2 * r, dz=4 * c, dk=d))
            last[s, j] = one
        one.start()

    def close_relay(s, d):
        j = group.index((1, 1, d))
        relays2[s, d].wait_recv()
        last[s, j] = remote(
            legs2.at[s, d],
            outs[s].at[quarter(1, 0), :, block(k)],
            fi_s.at[s, j],
            fi_r.at[s, j],
            peer(dz=4, dk=d),
        )
        last[s, j].start()

    def gate_two(s, c):
        top = flip(zh, c)

        def apply(i, carry):
            fin[s, top, block(i), :] = jnp.dot(gate[block(i), :], x2[s, top], preferred_element_type=F32).astype(BF)
            return carry

        lax.fori_loop(0, 4, apply, 0)

    def swapped(s):
        for i in range(4):
            swaps[s, i].wait_recv()

    def outer(a, b):
        return lax.dot_general(a, b, (((1,), (1,)), ((), ())), preferred_element_type=F32)

    pairs = {}

    def half(i):
        return pl.ds(pl.multiple_of(i * 512, 512), 512)

    def env_blocks(e, left, right):
        def one(t, carry):
            d = lax.rem(t + 1, 4)
            da, db = lax.div(d, 2), lax.rem(d, 2)
            ia, ib = xa + da - 2 * xa * da, xb + db - 2 * xb * db
            lo, hi = left(ia, ib)
            cs[e, d] = (outer(lo, right(0, oth)) + outer(hi, right(1, oth))).astype(BF)
            keep = outer(lo, right(0, k)) + outer(hi, right(1, k))
            ac0[e, d] = keep[:, :256]
            ac1[e, d] = keep[:, 256:].reshape(2, 8, 2, 8, 256)
            return carry

        lax.fori_loop(0, 4, one, 0)
        for d in (1, 2, 3, 0):
            pairs[e, d] = remote(cs.at[e, d], cr.at[e, d], cs_s.at[e, d], cs_r.at[e, d], peer(dk=1))
            pairs[e, d].start()

    def env_one():
        env_blocks(
            0,
            lambda ia, ib: (sb[1, ia * 2 + ib], x2[1, ib, block(ia * 2 + k), :]),
            lambda m, h: x1[0, oth if m == 0 else k, half(h), :],
        )

    def env_two():
        env_blocks(
            1,
            lambda ia, ib: (fin[1, 0, block(ia * 2 + ib), :], fin[1, 1, block(ia * 2 + ib), :]),
            lambda m, h: x2[0, m, half(h), :],
        )

    xsend, ysend, ysend2, xsend2, zsend, csend = {}, {}, {}, {}, {}, {}

    def push(table, e, d, src, dst, send, recv, to):
        table[e, d] = remote(src.at[e, d - 1], dst.at[e, d - 1], send.at[e, d - 1], recv.at[e, d - 1], to)
        table[e, d].start()

    def wait_all(table, e):
        for d in (1, 2, 3):
            table[e, d].wait_recv()

    def rows_of(d):
        return flip(yh, d & 2), flip(yl, d & 1)

    def stage_one(e):
        for d in (2, 1, 3, 0):
            pairs[e, d].wait_recv()
            first_half = ac0[e, d] + cr[e, d, :, :256].astype(F32)
            if d:
                xs[e, d - 1] = first_half.astype(BF)
                push(xsend, e, d, xs, xr, xs_s, xs_r, peer(dx=d))
            else:
                ac0[e, 0] = first_half
            ac1[e, d] += cr[e, d, :, 256:].astype(F32).reshape(2, 8, 2, 8, 256)
        for d in (2, 1, 3):
            a, b = rows_of(d)
            for i in range(4):
                ys[e, d - 1, i] = ac1[e, i, a, :, b].reshape(64, 256).astype(BF)
            push(ysend, e, d, ys, yr, ys_s, ys_r, peer(dy=d))

    def stage_two(e):
        wait_all(xsend, e)
        total = ac0[e, 0]
        for j in range(3):
            total = total + xr[e, j].astype(F32)
        mid[e] = total.reshape(2, 8, 2, 8, 256)
        for d in (2, 1, 3):
            a, b = rows_of(d)
            ys2[e, d - 1] = mid[e, a, :, b].reshape(64, 256).astype(BF)
            push(ysend2, e, d, ys2, yr2, ys2_s, ys2_r, peer(dy=d))
        wait_all(ysend, e)
        for d in (2, 1, 3, 0):
            total = ac1[e, d, yh, :, yl].reshape(64, 256)
            for j in range(3):
                total = total + yr[e, j, d].astype(F32)
            if d:
                xs2[e, d - 1] = total.astype(BF)
                push(xsend2, e, d, xs2, xr2, xs2_s, xs2_r, peer(dx=d))
            else:
                zb[e, :, 8:, :] = total.reshape(8, 8, 256)

    def stage_z(e):
        wait_all(ysend2, e)
        total = mid[e, yh, :, yl].reshape(64, 256)
        for j in range(3):
            total = total + yr2[e, j].astype(F32)
        zb[e, :, :8, :] = total.reshape(8, 8, 256)
        wait_all(xsend2, e)
        total = zb[e, :, 8:, :].reshape(64, 256)
        for j in range(3):
            total = total + xr2[e, j].astype(F32)
        zb[e, :, 8:, :] = total.reshape(8, 8, 256)
        zs[e] = zb[e].astype(BF)
        for d in (4, 5, 3, 6, 2, 7, 1):
            zsend[e, d] = remote(
                zs.at[e, (flip(zh, d & 4) * 2 + flip(zm, d & 2)) * 2 + flip(zl, d & 1)],
                zr.at[e, d - 1],
                zs_s.at[e, d - 1],
                zs_r.at[e, d - 1],
                peer(dz=d),
            )
            zsend[e, d].start()

    def stage_core(e):
        for d in range(1, 8):
            zsend[e, d].wait_recv()
        total = zb[e, (zh * 2 + zm) * 2 + zl]
        for d in range(7):
            total = total + zr[e, d].astype(F32)
        total = total * scale
        for j in range(4):
            q, c = j // 2, j % 2
            fb[e, j * 8 : j * 8 + 8, :] = total[q * 8 : q * 8 + 8, c * 128 : c * 128 + 128]
        for j in range(4):
            lc[e, j * 4 : j * 4 + 4, :] = fb[e, pl.ds(j * 8 + oth * 4, 4), :]
            env_outs[e][pl.ds(k * 4 + j, 4, stride=8), :] = fb[e, pl.ds(j * 8 + k * 4, 4), :]
        csend[e] = remote(lc.at[e], lr.at[e], lc_s.at[e], lc_r.at[e], peer(dk=1))
        csend[e].start()

    def stage_end(e):
        csend[e].wait_recv()
        for j in range(4):
            env_outs[e][pl.ds(oth * 4 + j, 4, stride=8), :] = lr[e, j * 4 : j * 4 + 4, :]

    gather(0, -1)
    gather(1, -1)
    loads[0].wait()
    gather(0, 2)
    gather(0, 0)
    gather(0, 1)
    gate_one(0)
    swapped(0)
    gate_two(0, 1)
    close(0, 0, 1, 0)
    close(0, 0, 1, 1)
    close_leg(0)
    gate_two(0, 0)
    for r, d in ((1, 0), (1, 1), (0, 1), (0, 0)):
        close(0, r, 0, d)
    gather(1, 2)
    close_relay(0, 0)
    close_relay(0, 1)
    gather(1, 0)
    gather(1, 1)
    gate_one(1)
    env_one()
    swapped(1)
    gate_two(1, 1)
    close(1, 0, 1, 0)
    close(1, 0, 1, 1)
    close_leg(1)
    gate_two(1, 0)
    stage_one(0)
    env_two()
    close_relay(1, 0)
    stage_one(1)
    stage_two(0)
    stage_two(1)
    for r, d in ((1, 0), (1, 1), (0, 1), (0, 0)):
        close(1, r, 0, d)
    stage_z(0)
    stage_z(1)
    close_relay(1, 1)
    stage_core(0)
    stage_core(1)
    stage_end(0)
    stage_end(1)
    for one in last.values():
        one.wait_recv()
    for one in homes:
        one.wait()
    for sent in (first, relays, relays2, swaps, last, pairs, xsend, ysend, ysend2, xsend2, zsend, csend):
        for one in sent.values():
            one.wait_send()


def lay_out(f_in, a_in, e1_in, e2_in, f_out, a_out, e1_out, e2_out, grid, tmp, flat, env, in_sem, out_sem):
    ins, outs = [], []
    for s, ref in enumerate((f_in, a_in)):
        for p in range(4):
            ins.append(pltpu.make_async_copy(ref.at[p], grid.at[s, p], in_sem.at[s * 4 + p]))
    for e, ref in enumerate((e1_in, e2_in)):
        ins.append(pltpu.make_async_copy(ref, env.at[e], in_sem.at[8 + e]))
    for one in ins:
        one.start()
    for s, ref in enumerate((f_out, a_out)):
        for p in range(4):
            ins[s * 4 + p].wait()
            for m in range(4):
                tmp[p % 2, pl.ds(m, 256, stride=4), :] = grid[s, p, :, m * 128 : m * 128 + 128].astype(F32)
            flat[s, p] = tmp[p % 2].astype(BF)
            outs.append(pltpu.make_async_copy(flat.at[s, p], ref.at[p], out_sem.at[s * 4 + p]))
            outs[-1].start()
    for e, ref in enumerate((e1_out, e2_out)):
        ins[8 + e].wait()
        outs.append(pltpu.make_async_copy(env.at[e], ref, out_sem.at[8 + e]))
        outs[-1].start()
    for one in outs:
        one.wait()


def on_device(forward_state, adjoint_state, gate_matrix):
    scale = 1.0 / math.sqrt(lax.axis_size("row") * lax.axis_size("col") * forward_state.shape[0] / gate_matrix.shape[0])
    dma = pltpu.SemaphoreType.DMA
    any_space = pl.BlockSpec(memory_space=pl.ANY)
    vmem = pl.BlockSpec(memory_space=pltpu.VMEM)
    scratch = [
        ((1024, 1024), BF),
        ((2, 4, 1024, 128), BF),
        ((2, 1024, 128), BF),
        ((2, 2, 256, 256), BF),
        ((1024, 128), F32),
        ((2, 2, 1024, 256), BF),
        ((2, 2, 1024, 256), BF),
        ((2, 4, 256, 256), BF),
        ((2, 2, 1024, 256), BF),
        ((2, 4, 256, 256), F32),
        ((2, 4, 2, 8, 2, 8, 256), F32),
        ((2, 2, 8, 2, 8, 256), F32),
        ((2, 4, 256, 512), BF),
        ((2, 4, 256, 512), BF),
        ((2, 3, 256, 256), BF),
        ((2, 3, 256, 256), BF),
        ((2, 3, 4, 64, 256), BF),
        ((2, 3, 4, 64, 256), BF),
        ((2, 3, 64, 256), BF),
        ((2, 3, 64, 256), BF),
        ((2, 3, 64, 256), BF),
        ((2, 3, 64, 256), BF),
        ((2, 8, 16, 256), F32),
        ((2, 8, 16, 256), BF),
        ((2, 7, 16, 256), BF),
        ((2, 32, 128), F32),
        ((2, 16, 128), F32),
        ((2, 16, 128), F32),
    ]
    sems = [(3,), (2,)]
    for shape in ((2, 3), (2,), (2, 2), (2, 4), (2, 7), (2, 4), (2, 3), (2, 3), (2, 3), (2, 3), (2, 7), (2,)):
        sems += [shape, shape]
    outs = pl.pallas_call(
        lambda *refs: kernel(scale, *refs),
        out_shape=[
            jax.ShapeDtypeStruct((4, 256, 512), BF),
            jax.ShapeDtypeStruct((4, 256, 512), BF),
            jax.ShapeDtypeStruct((32, 128), F32),
            jax.ShapeDtypeStruct((32, 128), F32),
        ],
        in_specs=[any_space] * 3,
        out_specs=[any_space, any_space, vmem, vmem],
        scratch_shapes=[pltpu.VMEM(shape, kind) for shape, kind in scratch] + [dma(shape) for shape in sems],
        compiler_params=pltpu.CompilerParams(collective_id=0, has_side_effects=True),
        name="step",
    )(forward_state.reshape(4, 1024, 128), adjoint_state.reshape(4, 1024, 128), gate_matrix)
    outs = pl.pallas_call(
        lay_out,
        out_shape=[jax.ShapeDtypeStruct((4, 1024, 128), BF)] * 2 + [jax.ShapeDtypeStruct((32, 128), F32)] * 2,
        in_specs=[any_space] * 4,
        out_specs=[any_space] * 4,
        scratch_shapes=[
            pltpu.VMEM((2, 4, 256, 512), BF),
            pltpu.VMEM((2, 1024, 128), F32),
            pltpu.VMEM((2, 4, 1024, 128), BF),
            pltpu.VMEM((2, 32, 128), F32),
            dma((10,)),
            dma((10,)),
        ],
        name="lay_out",
    )(*outs)
    return tuple(one.reshape(-1) for one in outs)


def solution(mesh):
    spec = P(("row", "col"))
    return jax.shard_map(
        on_device, mesh=mesh, in_specs=(spec, spec, P()), out_specs=(spec, spec, spec, spec), check_vma=False
    )
```

```python
import math

import jax
import jax.numpy as jnp
from jax import lax
from jax.experimental import pallas as pl
from jax.experimental.pallas import tpu as pltpu
from jax.sharding import PartitionSpec as P

MESH = pl.DeviceIdType.MESH
BF = jnp.bfloat16
F32 = jnp.float32


def flip(bit, by):
    return 1 - bit if by else bit


def kernel(
    scale, f_in, a_in, g_in, f_out, a_out, e1_out, e2_out,
    gate, flat, legs, legs2, tmp, x1, x2, sb, fin, ac0, ac1, mid, cs, cr, xs, xr, ys, yr, ys2, yr2, xs2, xr2, zb, zs, zr, fb, lc, lr,
    load_sem, home_sem, ex_s, ex_r, le_s, le_r, le2_s, le2_r, co_s, co_r, fi_s, fi_r, cs_s, cs_r, xs_s, xs_r, ys_s, ys_r,
    ys2_s, ys2_r, xs2_s, xs2_r, zs_s, zs_r, lc_s, lc_r,
):
    row, col = lax.axis_index("row"), lax.axis_index("col")
    xa, xb, yh = lax.div(row, 4), lax.rem(lax.div(row, 2), 2), lax.rem(row, 2)
    zh, zm, zl = lax.div(col, 16), lax.rem(lax.div(col, 8), 2), lax.rem(lax.div(col, 4), 2)
    yl, k = lax.rem(lax.div(col, 2), 2), lax.rem(col, 2)
    oth = 1 - k

    def peer(dx=0, dy=0, dz=0, dk=0):
        return {
            "row": (flip(xa, dx & 2) * 2 + flip(xb, dx & 1)) * 2 + flip(yh, dy & 2),
            "col": ((flip(zh, dz & 4) * 2 + flip(zm, dz & 2)) * 2 + flip(zl, dz & 1)) * 4
            + flip(yl, dy & 1) * 2
            + flip(k, dk),
        }

    def remote(src, dst, send, recv, to):
        return pltpu.make_async_remote_copy(
            src_ref=src, dst_ref=dst, send_sem=send, recv_sem=recv, device_id=to, device_id_type=MESH
        )

    ins, outs, env_outs = (f_in, a_in), (f_out, a_out), (e1_out, e2_out)
    home = yh * 2 + zh

    group = [(r, c, d) for r in (0, 1) for c in (1, 0) for d in (0, 1) if r + c + d]
    friends = [peer(dy=2 * r, dz=4 * c, dk=d) for r, c, d in group if r + c < 2]
    friends += [peer(dx=d) for d in (1, 2, 3)] + [peer(dy=d) for d in (1, 3)]
    friends += [peer(dz=d) for d in (1, 2, 3, 5, 6, 7)]
    barrier = pltpu.get_barrier_semaphore()
    for friend in friends:
        pl.semaphore_signal(barrier, inc=1, device_id=friend, device_id_type=MESH)

    loads = [pltpu.make_async_copy(g_in, gate, load_sem.at[2])]
    for s in (0, 1):
        loads.append(pltpu.make_async_copy(ins[s].at[home], flat.at[s, home], load_sem.at[s]))
    for one in loads:
        one.start()
    pl.semaphore_wait(barrier, len(friends))

    steps = ((0, 1), (1, 1), (1, 0))
    first, relays = {}, {}

    def quarter(r, c):
        return flip(yh, r) * 2 + flip(zh, c)

    def open_leg(s):
        relays[s] = remote(ins[s].at[quarter(1, 1)], legs.at[s], le_s.at[s], le_r.at[s], peer(dy=2))
        relays[s].start()

    def open_direct(s, j):
        r, c = steps[j]
        first[s, j] = remote(
            ins[s].at[quarter(r, c)], flat.at[s, home], ex_s.at[s, j], ex_r.at[s, j], peer(dy=2 * r, dz=4 * c)
        )
        first[s, j].start()

    def open_relay(s):
        relays[s].wait_recv()
        first[s, 1] = remote(legs.at[s], flat.at[s, quarter(1, 0)], ex_s.at[s, 1], ex_r.at[s, 1], peer(dz=4))
        first[s, 1].start()

    open_direct(0, 0)
    open_leg(0)
    open_leg(1)
    open_direct(0, 2)
    open_direct(1, 2)
    open_direct(1, 0)
    open_relay(0)
    open_relay(1)

    def untangle(s, slot):
        tmp[...] = flat[s, slot].astype(F32)
        rows = pl.ds(pl.multiple_of(slot * 256, 256), 256)
        for m in range(4):
            x1[s, m // 2, rows, (m % 2) * 128 : (m % 2) * 128 + 128] = tmp[pl.ds(m, 256, stride=4), :].astype(BF)

    def gather(s, j):
        if j < 0:
            loads[1 + s].wait()
            untangle(s, home)
        else:
            first[s, j].wait_recv()
            untangle(s, quarter(*steps[j]))

    def block(i):
        return pl.ds(pl.multiple_of(i * 256, 256), 256)

    swaps = {}

    def gate_one(s):
        def other(i, carry):
            sb[s, i] = jnp.dot(gate[block(i), :], x1[s, oth], preferred_element_type=F32).astype(BF)
            return carry

        lax.fori_loop(0, 4, other, 0)
        for i in range(4):
            swaps[s, i] = remote(
                sb.at[s, i],
                x2.at[s, i % 2, block((i // 2) * 2 + k), :],
                co_s.at[s, i],
                co_r.at[s, i],
                peer(dk=1),
            )
            swaps[s, i].start()

        def own(i, carry):
            x2[s, lax.rem(i, 2), block(lax.div(i, 2) * 2 + k), :] = jnp.dot(
                gate[block(i), :], x1[s, k], preferred_element_type=F32
            ).astype(BF)
            return carry

        lax.fori_loop(0, 4, own, 0)

    last, relays2, homes = {}, {}, []

    def piece(s, r, c, d):
        return fin.at[s, flip(zh, c), block(flip(yh, r) * 2 + flip(k, d)), :]

    def close_leg(s):
        for d in (0, 1):
            relays2[s, d] = remote(piece(s, 1, 1, d), legs2.at[s, d], le2_s.at[s, d], le2_r.at[s, d], peer(dy=2))
            relays2[s, d].start()

    def close(s, r, c, d):
        dst = outs[s].at[home, :, block(k)]
        if r + c + d == 0:
            one = pltpu.make_async_copy(piece(s, r, c, d), dst, home_sem.at[s])
            homes.append(one)
        else:
            j = group.index((r, c, d))
            one = remote(piece(s, r, c, d), dst, fi_s.at[s, j], fi_r.at[s, j], peer(dy=2 * r, dz=4 * c, dk=d))
            last[s, j] = one
        one.start()

    def close_relay(s, d):
        j = group.index((1, 1, d))
        relays2[s, d].wait_recv()
        last[s, j] = remote(
            legs2.at[s, d],
            outs[s].at[quarter(1, 0), :, block(k)],
            fi_s.at[s, j],
            fi_r.at[s, j],
            peer(dz=4, dk=d),
        )
        last[s, j].start()

    def gate_two(s, c):
        top = flip(zh, c)

        def apply(i, carry):
            fin[s, top, block(i), :] = jnp.dot(gate[block(i), :], x2[s, top], preferred_element_type=F32).astype(BF)
            return carry

        lax.fori_loop(0, 4, apply, 0)

    def swapped(s):
        for i in range(4):
            swaps[s, i].wait_recv()

    def outer(a, b):
        return lax.dot_general(a, b, (((1,), (1,)), ((), ())), preferred_element_type=F32)

    pairs = {}

    def half(i):
        return pl.ds(pl.multiple_of(i * 512, 512), 512)

    def env_blocks(e, left, right):
        def one(t, carry):
            d = lax.rem(t + 1, 4)
            da, db = lax.div(d, 2), lax.rem(d, 2)
            ia, ib = xa + da - 2 * xa * da, xb + db - 2 * xb * db
            lo, hi = left(ia, ib)
            cs[e, d] = (outer(lo, right(0, oth)) + outer(hi, right(1, oth))).astype(BF)
            keep = outer(lo, right(0, k)) + outer(hi, right(1, k))
            ac0[e, d] = keep[:, :256]
            ac1[e, d] = keep[:, 256:].reshape(2, 8, 2, 8, 256)
            return carry

        lax.fori_loop(0, 4, one, 0)
        for d in (1, 2, 3, 0):
            pairs[e, d] = remote(cs.at[e, d], cr.at[e, d], cs_s.at[e, d], cs_r.at[e, d], peer(dk=1))
            pairs[e, d].start()

    def env_one():
        env_blocks(
            0,
            lambda ia, ib: (sb[1, ia * 2 + ib], x2[1, ib, block(ia * 2 + k), :]),
            lambda m, h: x1[0, oth if m == 0 else k, half(h), :],
        )

    def env_two():
        env_blocks(
            1,
            lambda ia, ib: (fin[1, 0, block(ia * 2 + ib), :], fin[1, 1, block(ia * 2 + ib), :]),
            lambda m, h: x2[0, m, half(h), :],
        )

    xsend, ysend, ysend2, xsend2, zsend, csend = {}, {}, {}, {}, {}, {}

    def push(table, e, d, src, dst, send, recv, to):
        table[e, d] = remote(src.at[e, d - 1], dst.at[e, d - 1], send.at[e, d - 1], recv.at[e, d - 1], to)
        table[e, d].start()

    def wait_all(table, e):
        for d in (1, 2, 3):
            table[e, d].wait_recv()

    def rows_of(d):
        return flip(yh, d & 2), flip(yl, d & 1)

    def stage_one(e):
        for d in (2, 1, 3, 0):
            pairs[e, d].wait_recv()
            first_half = ac0[e, d] + cr[e, d, :, :256].astype(F32)
            if d:
                xs[e, d - 1] = first_half.astype(BF)
                push(xsend, e, d, xs, xr, xs_s, xs_r, peer(dx=d))
            else:
                ac0[e, 0] = first_half
            ac1[e, d] += cr[e, d, :, 256:].astype(F32).reshape(2, 8, 2, 8, 256)
        for d in (2, 1, 3):
            a, b = rows_of(d)
            for i in range(4):
                ys[e, d - 1, i] = ac1[e, i, a, :, b].reshape(64, 256).astype(BF)
            push(ysend, e, d, ys, yr, ys_s, ys_r, peer(dy=d))

    def stage_two(e):
        wait_all(xsend, e)
        total = ac0[e, 0]
        for j in range(3):
            total = total + xr[e, j].astype(F32)
        mid[e] = total.reshape(2, 8, 2, 8, 256)
        for d in (2, 1, 3):
            a, b = rows_of(d)
            ys2[e, d - 1] = mid[e, a, :, b].reshape(64, 256).astype(BF)
            push(ysend2, e, d, ys2, yr2, ys2_s, ys2_r, peer(dy=d))
        wait_all(ysend, e)
        for d in (2, 1, 3, 0):
            total = ac1[e, d, yh, :, yl].reshape(64, 256)
            for j in range(3):
                total = total + yr[e, j, d].astype(F32)
            if d:
                xs2[e, d - 1] = total.astype(BF)
                push(xsend2, e, d, xs2, xr2, xs2_s, xs2_r, peer(dx=d))
            else:
                zb[e, :, 8:, :] = total.reshape(8, 8, 256)

    def stage_z(e):
        wait_all(ysend2, e)
        total = mid[e, yh, :, yl].reshape(64, 256)
        for j in range(3):
            total = total + yr2[e, j].astype(F32)
        zb[e, :, :8, :] = total.reshape(8, 8, 256)
        wait_all(xsend2, e)
        total = zb[e, :, 8:, :].reshape(64, 256)
        for j in range(3):
            total = total + xr2[e, j].astype(F32)
        zb[e, :, 8:, :] = total.reshape(8, 8, 256)
        zs[e] = zb[e].astype(BF)
        for d in (4, 5, 3, 6, 2, 7, 1):
            zsend[e, d] = remote(
                zs.at[e, (flip(zh, d & 4) * 2 + flip(zm, d & 2)) * 2 + flip(zl, d & 1)],
                zr.at[e, d - 1],
                zs_s.at[e, d - 1],
                zs_r.at[e, d - 1],
                peer(dz=d),
            )
            zsend[e, d].start()

    def stage_core(e):
        for d in range(1, 8):
            zsend[e, d].wait_recv()
        total = zb[e, (zh * 2 + zm) * 2 + zl]
        for d in range(7):
            total = total + zr[e, d].astype(F32)
        total = total * scale
        for j in range(4):
            q, c = j // 2, j % 2
            fb[e, j * 8 : j * 8 + 8, :] = total[q * 8 : q * 8 + 8, c * 128 : c * 128 + 128]
        for j in range(4):
            lc[e, j * 4 : j * 4 + 4, :] = fb[e, pl.ds(j * 8 + oth * 4, 4), :]
            env_outs[e][pl.ds(k * 4 + j, 4, stride=8), :] = fb[e, pl.ds(j * 8 + k * 4, 4), :]
        csend[e] = remote(lc.at[e], lr.at[e], lc_s.at[e], lc_r.at[e], peer(dk=1))
        csend[e].start()

    def stage_end(e):
        csend[e].wait_recv()
        for j in range(4):
            env_outs[e][pl.ds(oth * 4 + j, 4, stride=8), :] = lr[e, j * 4 : j * 4 + 4, :]

    gather(0, -1)
    gather(1, -1)
    loads[0].wait()
    gather(0, 2)
    gather(0, 0)
    gather(0, 1)
    gate_one(0)
    swapped(0)
    gate_two(0, 1)
    close(0, 0, 1, 0)
    close(0, 0, 1, 1)
    close_leg(0)
    gate_two(0, 0)
    for r, d in ((1, 0), (1, 1), (0, 1), (0, 0)):
        close(0, r, 0, d)
    gather(1, 2)
    close_relay(0, 0)
    close_relay(0, 1)
    gather(1, 0)
    gather(1, 1)
    gate_one(1)
    env_one()
    swapped(1)
    gate_two(1, 1)
    close(1, 0, 1, 0)
    close(1, 0, 1, 1)
    close_leg(1)
    gate_two(1, 0)
    stage_one(0)
    env_two()
    close_relay(1, 0)
    stage_one(1)
    stage_two(0)
    stage_two(1)
    for r, d in ((1, 0), (1, 1), (0, 1), (0, 0)):
        close(1, r, 0, d)
    stage_z(0)
    stage_z(1)
    close_relay(1, 1)
    stage_core(0)
    stage_core(1)
    stage_end(0)
    stage_end(1)
    for one in last.values():
        one.wait_recv()
    for one in homes:
        one.wait()
    for sent in (first, relays, relays2, swaps, last, pairs, xsend, ysend, ysend2, xsend2, zsend, csend):
        for one in sent.values():
            one.wait_send()


def lay_out(f_in, a_in, e1_in, e2_in, f_out, a_out, e1_out, e2_out, grid, tmp, flat, env, in_sem, out_sem):
    ins, outs = [], []
    for s, ref in enumerate((f_in, a_in)):
        for p in range(4):
            ins.append(pltpu.make_async_copy(ref.at[p], grid.at[s, p], in_sem.at[s * 4 + p]))
    for e, ref in enumerate((e1_in, e2_in)):
        ins.append(pltpu.make_async_copy(ref, env.at[e], in_sem.at[8 + e]))
    for one in ins:
        one.start()
    for s, ref in enumerate((f_out, a_out)):
        for p in range(4):
            ins[s * 4 + p].wait()
            for m in range(4):
                tmp[p % 2, pl.ds(m, 256, stride=4), :] = grid[s, p, :, m * 128 : m * 128 + 128].astype(F32)
            flat[s, p] = tmp[p % 2].astype(BF)
            outs.append(pltpu.make_async_copy(flat.at[s, p], ref.at[p], out_sem.at[s * 4 + p]))
            outs[-1].start()
    for e, ref in enumerate((e1_out, e2_out)):
        ins[8 + e].wait()
        outs.append(pltpu.make_async_copy(env.at[e], ref, out_sem.at[8 + e]))
        outs[-1].start()
    for one in outs:
        one.wait()


def on_device(forward_state, adjoint_state, gate_matrix):
    scale = 1.0 / math.sqrt(lax.axis_size("row") * lax.axis_size("col") * forward_state.shape[0] / gate_matrix.shape[0])
    dma = pltpu.SemaphoreType.DMA
    any_space = pl.BlockSpec(memory_space=pl.ANY)
    vmem = pl.BlockSpec(memory_space=pltpu.VMEM)
    scratch = [
        ((1024, 1024), BF),
        ((2, 4, 1024, 128), BF),
        ((2, 1024, 128), BF),
        ((2, 2, 256, 256), BF),
        ((1024, 128), F32),
        ((2, 2, 1024, 256), BF),
        ((2, 2, 1024, 256), BF),
        ((2, 4, 256, 256), BF),
        ((2, 2, 1024, 256), BF),
        ((2, 4, 256, 256), F32),
        ((2, 4, 2, 8, 2, 8, 256), F32),
        ((2, 2, 8, 2, 8, 256), F32),
        ((2, 4, 256, 512), BF),
        ((2, 4, 256, 512), BF),
        ((2, 3, 256, 256), BF),
        ((2, 3, 256, 256), BF),
        ((2, 3, 4, 64, 256), BF),
        ((2, 3, 4, 64, 256), BF),
        ((2, 3, 64, 256), BF),
        ((2, 3, 64, 256), BF),
        ((2, 3, 64, 256), BF),
        ((2, 3, 64, 256), BF),
        ((2, 8, 16, 256), F32),
        ((2, 8, 16, 256), BF),
        ((2, 7, 16, 256), BF),
        ((2, 32, 128), F32),
        ((2, 16, 128), F32),
        ((2, 16, 128), F32),
    ]
    sems = [(3,), (2,)]
    for shape in ((2, 3), (2,), (2, 2), (2, 4), (2, 7), (2, 4), (2, 3), (2, 3), (2, 3), (2, 3), (2, 7), (2,)):
        sems += [shape, shape]
    outs = pl.pallas_call(
        lambda *refs: kernel(scale, *refs),
        out_shape=[
            jax.ShapeDtypeStruct((4, 256, 512), BF),
            jax.ShapeDtypeStruct((4, 256, 512), BF),
            jax.ShapeDtypeStruct((32, 128), F32),
            jax.ShapeDtypeStruct((32, 128), F32),
        ],
        in_specs=[pl.BlockSpec(memory_space=pltpu.HBM)] * 3,
        out_specs=[any_space, any_space, vmem, vmem],
        scratch_shapes=[pltpu.VMEM(shape, kind) for shape, kind in scratch] + [dma(shape) for shape in sems],
        compiler_params=pltpu.CompilerParams(collective_id=0, has_side_effects=True, vmem_limit_bytes=36 << 20),
        name="step",
    )(
        pltpu.with_memory_space_constraint(forward_state.reshape(4, 1024, 128), pltpu.HBM),
        pltpu.with_memory_space_constraint(adjoint_state.reshape(4, 1024, 128), pltpu.HBM),
        pltpu.with_memory_space_constraint(gate_matrix, pltpu.HBM),
    )
    outs = pl.pallas_call(
        lay_out,
        out_shape=[jax.ShapeDtypeStruct((4, 1024, 128), BF)] * 2 + [jax.ShapeDtypeStruct((32, 128), F32)] * 2,
        in_specs=[any_space] * 4,
        out_specs=[any_space] * 4,
        scratch_shapes=[
            pltpu.VMEM((2, 4, 256, 512), BF),
            pltpu.VMEM((2, 1024, 128), F32),
            pltpu.VMEM((2, 4, 1024, 128), BF),
            pltpu.VMEM((2, 32, 128), F32),
            dma((10,)),
            dma((10,)),
        ],
        compiler_params=pltpu.CompilerParams(vmem_limit_bytes=16 << 20),
        name="lay_out",
    )(*outs)
    return tuple(one.reshape(-1) for one in outs)


def solution(mesh):
    spec = P(("row", "col"))
    return jax.shard_map(
        on_device, mesh=mesh, in_specs=(spec, spec, P()), out_specs=(spec, spec, spec, spec), check_vma=False
    )
```
